32 devices in a mesh: wide: 8 (over z, y), narrow: 4 (over x, core).
Axes of the slice: x: 2, y: 2, z: 4, core: 2. Of those that a mesh axis runs over, the one named last changes fastest.
Arguments:
- features: bfloat16 [131072, 512], P(('wide', 'narrow'))
- coefficients: float32 [131072, 128], P(('wide', 'narrow')), may hold values from -0.12 to 0.12
- targets: bfloat16 [131072, 128], P(('wide', 'narrow')), may hold values from -6 to 6
- block_rows: int32 [2, 512], replicated, may hold values from 0 to 4095, as said below
- block_owner: int32 [2], replicated, may hold values from 0 to 31, as said below
Outputs:
- new_coefficients: float32 [131072, 128], P(('wide', 'narrow'))
The draws below stay inside these ranges and needn't reach their ends.
Inputs may be any that keep to these rules, and one draw needn't show every extreme that they name: `block_rows`: each row lists 512 distinct local rows of the shard of device block_owner[i]. `block_owner`: the 2 owners are distinct and one of them is the last device; device number d holds samples d * 4096 to (d + 1) * 4096 - 1, d being its wide index times the narrow axis's size plus its narrow index.
All inputs are finite; a program needn't handle non-finite values.
Results may differ from the reference program's by a relative error of at most 0.0023.
Values may be sent and summed in bfloat16 or wider, within the bound.
A program may use at most 64 MiB of HBM per device.

```python
import math
import jax
import jax.numpy as jnp
from jax import lax

FEAT = 512
OUT = 128
BLOCK = 512
ITERS = 2
ROWS_DEV = 4096
SAMPLES = 131072


def draw_features(key, part):
    key_list = jax.random.split(jax.random.fold_in(key, 17), 5)
    latent = jax.random.uniform(key_list[0], (SAMPLES, 2), jnp.float32, -4.0, 4.0)
    frequency = jax.random.normal(key_list[1], (2, FEAT), jnp.float32)
    offsets = jax.random.uniform(key_list[2], (FEAT,), jnp.float32, 0.0, 2.0 * math.pi)
    angles = latent[:, 0:1] * frequency[0] + latent[:, 1:2] * frequency[1] + offsets
    jitter = 0.5 * jax.random.normal(key_list[4], (SAMPLES, FEAT), jnp.float32)
    values = math.sqrt(2.0) * jnp.cos(angles) + jitter
    return values.astype(jnp.bfloat16)


def draw_block_rows(key, part):
    base_key = jax.random.fold_in(key, 23)
    listing = []
    for iteration in range(ITERS):
        subkeys = jax.random.split(jax.random.fold_in(base_key, iteration))
        if iteration == 0:
            middle = jax.random.permutation(subkeys[0], ROWS_DEV - 2)[:BLOCK - 2].astype(jnp.int32) + 1
            chosen = jnp.concatenate([jnp.array([0, ROWS_DEV - 1], jnp.int32), middle])
            listing.append(jax.random.permutation(subkeys[1], chosen).astype(jnp.int32))
        else:
            listing.append(jax.random.permutation(subkeys[0], ROWS_DEV)[:BLOCK].astype(jnp.int32))
    return jnp.stack(listing)


def draw_block_owner(key, part):
    owner_keys = jax.random.split(jax.random.fold_in(key, 29))
    device_count = SAMPLES // ROWS_DEV
    others = jax.random.permutation(owner_keys[0], device_count - 1)[:ITERS].astype(jnp.int32)
    position = jax.random.randint(owner_keys[1], (), 0, ITERS)
    slots = jnp.arange(ITERS, dtype=jnp.int32)
    return jnp.where(slots == position, jnp.int32(device_count - 1), others).astype(jnp.int32)


def shard_levels(own_key, extent, shards, least, high):
    loudness, own = 1.0, jax.random.fold_in(own_key, 6)
    for dim, shards_of in shards:
        steps = jnp.exp(jax.random.uniform(jax.random.fold_in(own, dim), (shards_of,), jnp.float32, least / len(shards), high / len(shards)))
        loudness = loudness * jnp.repeat(steps, extent[dim] // shards_of).reshape([-1 if axis == dim else 1 for axis in range(len(extent))])
    return loudness


def scatter_about(rng, shape, deviation, bound, cuts=(), held_as=jnp.bfloat16):
    values = jax.random.normal(rng, shape, jnp.float32) * deviation
    if len(cuts) > 0:
        values = shard_levels(rng, shape, cuts, -0.22, 0.18) * values
    return jnp.clip(values, min=-bound, max=bound).astype(held_as)


def setup_inputs(seed: int = 0) -> dict:
    key_of = jax.random.split(jax.random.key(seed), 6)
    return {
        "features": draw_features(jax.random.fold_in(key_of[5], 71), 0),
        "coefficients": scatter_about(key_of[1], (SAMPLES, OUT), 0.02, 0.12, ((0, 32),), jnp.float32),
        "targets": scatter_about(key_of[2], (SAMPLES, OUT), 1.0, 6.0, ((0, 32),)),
        "block_rows": draw_block_rows(jax.random.fold_in(key_of[5], 71), 0),
        "block_owner": draw_block_owner(jax.random.fold_in(key_of[5], 71), 0),
    }


ridge_term = 0.5

def square_sums(feature_rows):
    widened = feature_rows.astype(jnp.float32)
    return jnp.sum(widened * widened, axis=1)

def kernel_values(left_rows, left_squares, right_rows, right_squares):
    products = lax.dot_general(left_rows.astype(jnp.float32), right_rows.astype(jnp.float32), (((1,), (1,)), ((), ())), preferred_element_type=jnp.float32)
    distance = left_squares[:, None] + right_squares[None, :] - 2.0 * products
    return jnp.exp(-distance / left_rows.shape[1])

def cholesky_solve(block_feats, block_squares, right_side):
    gram_matrix = kernel_values(block_feats, block_squares, block_feats, block_squares)
    gram_matrix = gram_matrix + ridge_term * jnp.eye(block_feats.shape[0], dtype=jnp.float32)
    factor = jnp.linalg.cholesky(gram_matrix)
    lower_part = lax.linalg.triangular_solve(factor, right_side, left_side=True, lower=True)
    return lax.linalg.triangular_solve(factor, lower_part, left_side=True, lower=True, transpose_a=True)

def reference(features, coefficients, targets, block_rows, block_owner):
    squares = square_sums(features)
    shard_count = SAMPLES // ROWS_DEV
    feat_blocks = features.reshape(shard_count, ROWS_DEV, FEAT)
    square_blocks = squares.reshape(shard_count, ROWS_DEV)
    updated = coefficients
    for iteration in range(ITERS):
        global_rows = (block_owner[iteration] * ROWS_DEV + block_rows[iteration]).astype(jnp.int32)
        block_feats = features[global_rows]
        block_squares = squares[global_rows]
        masked = updated.at[global_rows].set(0.0).astype(jnp.bfloat16).reshape(shard_count, ROWS_DEV, OUT)

        def add_block(running, pieces):
            piece_feats, piece_squares, piece_weights = pieces
            kernel = kernel_values(block_feats, block_squares, piece_feats, piece_squares).astype(jnp.bfloat16)
            return (running + jnp.dot(kernel.astype(jnp.float32), piece_weights.astype(jnp.float32), preferred_element_type=jnp.float32), None)
        running, _ = lax.scan(add_block, jnp.zeros((BLOCK, OUT), jnp.float32), (feat_blocks, square_blocks, masked))
        right_side = targets[global_rows].astype(jnp.float32) - running
        solution = cholesky_solve(block_feats, block_squares, right_side)
        updated = updated.at[global_rows].set(solution)
    return updated
```

```python
import functools
import math

import jax
import jax.numpy as jnp
from jax import lax
from jax.experimental import pallas as pl
from jax.experimental.pallas import tpu as pltpu
from jax.sharding import PartitionSpec as P

ridge_term = 0.5
newton_steps = 8
f32 = jnp.float32
bf16 = jnp.bfloat16
whole_vmem = pl.BlockSpec(memory_space=pltpu.VMEM)
whole_smem = pl.BlockSpec(memory_space=pltpu.SMEM)


def nn_dot(left, right):
    return jnp.dot(left, right, preferred_element_type=f32)


def nt_dot(left, right):
    return lax.dot_general(left, right, (((1,), (1,)), ((), ())), preferred_element_type=f32)


def tn_dot(left, right):
    return lax.dot_general(left, right, (((0,), (0,)), ((), ())), preferred_element_type=f32)


def halves(value):
    high = value.astype(bf16)
    return high, (value - high.astype(f32)).astype(bf16)


def fine_dot(left, right, dot=nn_dot):
    left_high, left_low = halves(left)
    right_high, right_low = halves(right)
    return dot(left_high, right_high) + (dot(left_high, right_low) + dot(left_low, right_high))


def row_squares(rows):
    widened = rows.astype(f32)
    return jnp.sum(widened * widened, axis=1, keepdims=True)


def lane_squares(rows):
    widened = rows.astype(f32)
    high, low = halves(widened * widened)
    ones = jnp.ones((8, rows.shape[1]), bf16)
    return (nt_dot(ones, high) + nt_dot(ones, low))[0:1]


def gather_kernel(flags, rows_down, rows_across, feats, coefs, targs, spread_out, targ_out, mask0_out, mask1_out,
                  squares_out, feat_total, targ_total):
    step = pl.program_id(0)
    tile = feats.shape[0]
    block = rows_down.shape[0]
    first, second = flags[0], flags[1]
    squares_out[...] = lane_squares(feats[...])
    plain = coefs[...].astype(bf16)

    @pl.when(first + second == 0)
    def _():
        mask0_out[...] = plain
        mask1_out[...] = plain

        @pl.when(step == 0)
        def _():
            spread_out[...] = jnp.zeros_like(spread_out)
            targ_out[...] = jnp.zeros_like(targ_out)

    @pl.when(first + second > 0)
    def _():
        lanes = lax.broadcasted_iota(jnp.int32, (block, tile), 1) + step * tile
        pick = jnp.where(lanes == rows_down[...], 1.0, 0.0).astype(bf16)
        feat_part = nn_dot(pick, feats[...])
        targ_part = nn_dot(pick, targs[...])
        subs = lax.broadcasted_iota(jnp.int32, (tile, block), 0) + step * tile
        place = jnp.where(subs == rows_across[...], 1.0, 0.0).astype(bf16)
        taken = nn_dot(place, jnp.ones((block, coefs.shape[1]), bf16)) > 0.5
        cleared = jnp.where(taken, 0.0, coefs[...]).astype(bf16)
        mask0_out[...] = jnp.where(first > 0, cleared, plain)
        mask1_out[...] = cleared

        @pl.when(step == 0)
        def _():
            feat_total[...] = feat_part
            targ_total[...] = targ_part

        @pl.when(step > 0)
        def _():
            feat_total[...] += feat_part
            targ_total[...] += targ_part

        @pl.when(step == pl.num_programs(0) - 1)
        def _():
            for index, flag in enumerate((first, second)):
                keep = flag > 0
                spread_out[pl.ds(index * block, block), :] = jnp.where(keep, feat_total[...], 0.0).astype(bf16)
                targ_out[pl.ds(index * block, block), :] = jnp.where(keep, targ_total[...], 0.0)


def gather_own(flags, rows, features, coefficients, targets):
    count, width = features.shape
    outs = coefficients.shape[1]
    block = rows.shape[0]
    tile = min(1024, count)
    moving = lambda columns: pl.BlockSpec((tile, columns), lambda i: (i, 0))
    still = lambda shape: pl.BlockSpec(shape, lambda i: (0, 0))
    return pl.pallas_call(
        gather_kernel,
        grid=(count // tile,),
        in_specs=[whole_smem, still((block, 1)), still((1, block)), moving(width), moving(outs), moving(outs)],
        out_specs=[
            still((2 * block, width)), still((2 * block, outs)), moving(outs), moving(outs),
            pl.BlockSpec((1, tile), lambda i: (0, i)),
        ],
        out_shape=[
            jax.ShapeDtypeStruct((2 * block, width), bf16), jax.ShapeDtypeStruct((2 * block, outs), f32),
            jax.ShapeDtypeStruct((count, outs), bf16), jax.ShapeDtypeStruct((count, outs), bf16),
            jax.ShapeDtypeStruct((1, count), f32),
        ],
        scratch_shapes=[pltpu.VMEM((block, width), f32), pltpu.VMEM((block, outs), f32)],
        compiler_params=pltpu.CompilerParams(vmem_limit_bytes=40 << 20),
        name="gather_own",
    )(flags, rows[:, None], rows[None, :], features, coefficients, targets)


def terms_kernel(arrived, feats, squares, mask0, mask1, own, terms_out, offsets):
    step = pl.program_id(0)
    width = feats.shape[1]
    block = arrived.shape[0] // 2
    scale = math.log2(math.e) / width

    @pl.when(step == 0)
    def _():
        offsets[...] = row_squares(arrived[...]) * (-scale)
        terms_out[...] = own[...]

    beside = squares[...] * (-scale)
    piece = block // 2
    for part in range(4):
        span = pl.ds(part * piece, piece)
        products = nt_dot(arrived[span, :], feats[...])
        values = jnp.exp2(products * (2.0 * scale) + offsets[span, :] + beside).astype(bf16)
        mask = mask0 if part < 2 else mask1
        terms_out[span, :] -= nn_dot(values, mask[...])


def local_terms(arrived, features, squares, mask0, mask1, own):
    count, width = features.shape
    outs = own.shape[1]
    tile = min(1024, count)
    moving = lambda columns: pl.BlockSpec((tile, columns), lambda i: (i, 0))
    still = lambda shape: pl.BlockSpec(shape, lambda i: (0, 0))
    return pl.pallas_call(
        terms_kernel,
        grid=(count // tile,),
        in_specs=[
            still(arrived.shape), moving(width), pl.BlockSpec((1, tile), lambda i: (0, i)), moving(outs), moving(outs),
            still(own.shape),
        ],
        out_specs=still(own.shape),
        out_shape=jax.ShapeDtypeStruct(own.shape, f32),
        scratch_shapes=[pltpu.VMEM((arrived.shape[0], 1), f32)],
        compiler_params=pltpu.CompilerParams(vmem_limit_bytes=40 << 20),
        name="local_terms",
    )(arrived, features, squares, mask0, mask1, own)


def newton_plan(size):
    least, most = ridge_term * 0.96, size + ridge_term + 0.1
    radius = (most - least) / (most + least)
    start = 2.0 / (most + least)
    scales = []
    for _ in range(newton_steps):
        scales.append(2.0 / (2.0 - radius * radius))
        radius = radius * radius / (2.0 - radius * radius)
    return start, scales


def invert_pair(matrices, keep):
    size = matrices[0].shape[0]
    start, scales = newton_plan(size)
    eye = jnp.where(
        lax.broadcasted_iota(jnp.int32, (size, size), 0) == lax.broadcasted_iota(jnp.int32, (size, size), 1), 1.0, 0.0
    )
    for index, matrix in enumerate(matrices):
        keep[index] = (2.0 * start * scales[0]) * eye - (start * start * scales[0]) * matrix
    for scale in scales[1:]:
        guesses = [keep[index] for index in range(2)]
        rests = [fine_dot(matrix, guess) for matrix, guess in zip(matrices, guesses)]
        for index in range(2):
            change = fine_dot(guesses[index], rests[index])
            keep[index] = (2.0 * scale) * guesses[index] - scale * change


def factor_kernel(arrived, first_out, cross_out, second_out, between_out):
    width = arrived.shape[1]
    block = arrived.shape[0] // 2
    half = block // 2
    scale = math.log2(math.e) / width

    def values(left, right):
        left_rows, right_rows = arrived[left, :], arrived[right, :]
        distance = row_squares(left_rows) + lane_squares(right_rows) - 2.0 * nt_dot(left_rows, right_rows)
        return jnp.exp2(distance * (-scale))

    span = lambda index, part: pl.ds(index * block + part * half, half)
    ridge = jnp.where(
        lax.broadcasted_iota(jnp.int32, (half, half), 0) == lax.broadcasted_iota(jnp.int32, (half, half), 1),
        ridge_term, 0.0,
    )
    invert_pair([values(span(i, 0), span(i, 0)) + ridge for i in range(2)], first_out)
    rests = []
    for i in range(2):
        low = values(span(i, 1), span(i, 0))
        cross = fine_dot(low, first_out[i])
        cross_out[i] = cross
        rests.append(values(span(i, 1), span(i, 1)) + ridge - fine_dot(cross, low, nt_dot))
    invert_pair(rests, second_out)
    for part in range(2):
        between_out[pl.ds(part * half, half), :] = values(span(1, part), pl.ds(0, block)).astype(bf16)


def factor(arrived):
    block = arrived.shape[0] // 2
    half = block // 2
    shape = jax.ShapeDtypeStruct((2, half, half), f32)
    return pl.pallas_call(
        factor_kernel,
        in_specs=[whole_vmem],
        out_specs=[whole_vmem] * 4,
        out_shape=[shape, shape, shape, jax.ShapeDtypeStruct((block, block), bf16)],
        compiler_params=pltpu.CompilerParams(vmem_limit_bytes=40 << 20),
        name="factor",
    )(arrived)


def finish_kernel(flags, rows_across, coefs, sides, first_inv, cross, second_inv, between, out, pieces):
    step = pl.program_id(0)
    block = rows_across.shape[1]
    half = block // 2
    tile, outs = coefs.shape

    def solve(index, upper, lower):
        rest = lower - fine_dot(cross[index], upper)
        low_part = fine_dot(second_inv[index], rest)
        high_part = fine_dot(first_inv[index], upper) - fine_dot(cross[index], low_part, tn_dot)
        return high_part, low_part

    mine = flags[0] + flags[1] > 0

    @pl.when(mine & (step == 0))
    def _():
        fresh = solve(0, sides[pl.ds(0, half), :], sides[pl.ds(half, half), :])
        sent = jnp.concatenate([part.astype(bf16) for part in fresh], axis=0)
        moved = nn_dot(between[...], sent)
        later = solve(1, sides[pl.ds(block, half), :] - moved[:half], sides[pl.ds(block + half, half), :] - moved[half:])
        for part in range(2):
            value = jnp.where(flags[0] > 0, fresh[part], later[part])
            high = value.astype(bf16)
            rest = value - high.astype(f32)
            mid = rest.astype(bf16)
            low = (rest - mid.astype(f32)).astype(bf16)
            for index, piece in enumerate((high, mid, low)):
                pieces[pl.ds(part * half, half), pl.ds(index * outs, outs)] = piece
        pieces[:, pl.ds(3 * outs, outs)] = jnp.ones((block, outs), bf16)

    @pl.when(mine)
    def _():
        subs = lax.broadcasted_iota(jnp.int32, (tile, block), 0) + step * tile
        place = jnp.where(subs == rows_across[...], 1.0, 0.0).astype(bf16)
        spread = nn_dot(place, pieces[...])
        value = spread[:, :outs] + spread[:, outs : 2 * outs] + spread[:, 2 * outs : 3 * outs]
        out[...] = jnp.where(spread[:, 3 * outs :] > 0.5, value, coefs[...])

    @pl.when(jnp.logical_not(mine))
    def _():
        out[...] = coefs[...]


def finish(flags, rows, coefficients, sides, first_inv, cross, second_inv, between):
    count, outs = coefficients.shape
    block = rows.shape[0]
    tile = min(1024, count)
    moving = pl.BlockSpec((tile, outs), lambda i: (i, 0))
    return pl.pallas_call(
        finish_kernel,
        grid=(count // tile,),
        in_specs=[whole_smem, whole_vmem, moving] + [whole_vmem] * 5,
        out_specs=moving,
        out_shape=jax.ShapeDtypeStruct(coefficients.shape, f32),
        scratch_shapes=[pltpu.VMEM((block, 4 * outs), bf16)],
        compiler_params=pltpu.CompilerParams(vmem_limit_bytes=40 << 20),
        name="finish",
    )(flags, rows[None, :], coefficients, sides, first_inv, cross, second_inv, between)


def per_device(features, coefficients, targets, block_rows, block_owner):
    device = lax.axis_index("wide") * lax.axis_size("narrow") + lax.axis_index("narrow")
    flags = (block_owner == device).astype(jnp.int32)
    rows = jnp.where(flags[0] > 0, block_rows[0], block_rows[1])
    spread, own, mask0, mask1, squares = gather_own(flags, rows, features, coefficients, targets)
    arrived = lax.psum(spread, ("wide", "narrow"))
    terms = local_terms(arrived, features, squares, mask0, mask1, own)
    sides = lax.psum(terms, ("wide", "narrow"))
    parts = factor(arrived)
    return finish(flags, rows, coefficients, sides, *parts)


def solution(mesh):
    rows = P(("wide", "narrow"), None)
    return jax.shard_map(
        per_device,
        mesh=mesh,
        in_specs=(rows, rows, rows, P(), P()),
        out_specs=rows,
        check_vma=False,
    )
```

```python
import functools
import math

import jax
import jax.numpy as jnp
from jax import lax
from jax.experimental import pallas as pl
from jax.experimental.pallas import tpu as pltpu
from jax.sharding import PartitionSpec as P

ridge_term = 0.5
newton_steps = 8
f32 = jnp.float32
bf16 = jnp.bfloat16
whole_vmem = pl.BlockSpec(memory_space=pltpu.VMEM)
whole_smem = pl.BlockSpec(memory_space=pltpu.SMEM)


def nn_dot(left, right):
    return jnp.dot(left, right, preferred_element_type=f32)


def nt_dot(left, right):
    return lax.dot_general(left, right, (((1,), (1,)), ((), ())), preferred_element_type=f32)


def tn_dot(left, right):
    return lax.dot_general(left, right, (((0,), (0,)), ((), ())), preferred_element_type=f32)


def halves(value):
    high = value.astype(bf16)
    return high, (value - high.astype(f32)).astype(bf16)


def fine_dot(left, right, dot=nn_dot):
    left_high, left_low = halves(left)
    right_high, right_low = halves(right)
    return dot(left_high, right_high) + (dot(left_high, right_low) + dot(left_low, right_high))


def row_squares(rows):
    widened = rows.astype(f32)
    return jnp.sum(widened * widened, axis=1, keepdims=True)


def lane_squares(rows):
    widened = rows.astype(f32)
    high, low = halves(widened * widened)
    ones = jnp.ones((8, rows.shape[1]), bf16)
    return (nt_dot(ones, high) + nt_dot(ones, low))[0:1]


def cube_orders(wide, narrow):
    bits = [("narrow", 1 << k) for k in range(narrow.bit_length() - 1)]
    bits += [("wide", 1 << k) for k in range(wide.bit_length() - 1)]
    turned = bits[:1] + bits[2:-1] + bits[1:2] + bits[-1:]
    return bits, turned if len(bits) > 3 else bits


def cube_kernel(orders, value, out, *scratch):
    steps = len(orders[0])
    kept, sems = scratch[:-1], scratch[-1]
    chunks = 1 << steps

    def side(bit):
        axis, weight = bit
        return lax.rem(lax.axis_index(axis) // weight, 2)

    def partner(bit):
        axis, weight = bit
        place = {name: lax.axis_index(name) for name in ("wide", "narrow")}
        place[axis] = place[axis] + weight - 2 * weight * side(bit)
        return (place["wide"], place["narrow"])

    def copy(source, target, bit, part, step, phase):
        return pltpu.make_async_remote_copy(
            src_ref=source, dst_ref=target, send_sem=sems.at[0, phase, part, step], recv_sem=sems.at[1, phase, part, step],
            device_id=partner(bit), device_id_type=pl.DeviceIdType.MESH,
        )

    barrier = pltpu.get_barrier_semaphore()
    for bit in orders[0]:
        pl.semaphore_signal(barrier, inc=1, device_id=partner(bit), device_id_type=pl.DeviceIdType.MESH)
    pl.semaphore_wait(barrier, steps)

    def held(part, step):
        if step < 0:
            return value.at[pl.ds(part * chunks, chunks)]
        return kept[part * steps + step]

    started = []
    flying = {}

    def absorb(part, step):
        count = chunks >> (step + 1)
        flying[part].wait_recv()
        spot = held(part, step)
        spot[...] = spot[...] + held(part, step - 1)[pl.ds(side(orders[part][step]) * count, count)]

    for step in range(steps):
        count = chunks >> (step + 1)
        for part, order in enumerate(orders):
            if step > 0:
                absorb(part, step - 1)
            away = (1 - side(order[step])) * count
            flying[part] = copy(held(part, step - 1).at[pl.ds(away, count)], held(part, step), order[step], part, step, 0)
            flying[part].start()
            started.append(flying[part])
    bases = []
    for part, order in enumerate(orders):
        absorb(part, steps - 1)
        base = part * chunks
        listed = []
        for step in range(steps):
            base = base + side(order[step]) * (chunks >> (step + 1))
            listed.append(base)
        bases.append(listed)
        out[pl.ds(base, 1)] = held(part, steps - 1)[...]
    for step in reversed(range(steps)):
        count = chunks >> (step + 1)
        for part, order in enumerate(orders):
            if step < steps - 1:
                flying[part].wait_recv()
            span = out.at[pl.ds(bases[part][step], count)]
            flying[part] = copy(span, span, order[step], part, step, 1)
            flying[part].start()
            started.append(flying[part])
    for part in range(len(orders)):
        flying[part].wait_recv()
    for sent in started:
        sent.wait_send()


def cube_sum(value, wide, narrow, number):
    orders = cube_orders(wide, narrow)
    steps = len(orders[0])
    chunks = 1 << steps
    rows, columns = value.shape
    depth = rows // (2 * chunks)
    shape = (2 * chunks, depth, columns)
    slots = [pltpu.VMEM((chunks >> (step + 1), depth, columns), value.dtype) for _ in orders for step in range(steps)]
    summed = pl.pallas_call(
        functools.partial(cube_kernel, orders),
        in_specs=[whole_vmem],
        out_specs=whole_vmem,
        out_shape=jax.ShapeDtypeStruct(shape, value.dtype),
        scratch_shapes=slots + [pltpu.SemaphoreType.DMA((2, 2, 2, steps))],
        compiler_params=pltpu.CompilerParams(collective_id=number, has_side_effects=True, vmem_limit_bytes=40 << 20),
        name="cube_sum",
    )(value.reshape(shape))
    return summed.reshape(rows, columns)


def gather_kernel(flags, rows_down, rows_across, feats, coefs, targs, spread_out, targ_out, mask0_out, mask1_out,
                  squares_out, feat_total, targ_total):
    step = pl.program_id(0)
    tile = feats.shape[0]
    block = rows_down.shape[0]
    first, second = flags[0], flags[1]
    squares_out[...] = lane_squares(feats[...])
    plain = coefs[...].astype(bf16)

    @pl.when(first + second == 0)
    def _():
        mask0_out[...] = plain
        mask1_out[...] = plain

        @pl.when(step == 0)
        def _():
            spread_out[...] = jnp.zeros_like(spread_out)
            targ_out[...] = jnp.zeros_like(targ_out)

    @pl.when(first + second > 0)
    def _():
        lanes = lax.broadcasted_iota(jnp.int32, (block, tile), 1) + step * tile
        pick = jnp.where(lanes == rows_down[...], 1.0, 0.0).astype(bf16)
        feat_part = nn_dot(pick, feats[...])
        targ_part = nn_dot(pick, targs[...])
        subs = lax.broadcasted_iota(jnp.int32, (tile, block), 0) + step * tile
        place = jnp.where(subs == rows_across[...], 1.0, 0.0).astype(bf16)
        taken = nn_dot(place, jnp.ones((block, coefs.shape[1]), bf16)) > 0.5
        cleared = jnp.where(taken, 0.0, coefs[...]).astype(bf16)
        mask0_out[...] = jnp.where(first > 0, cleared, plain)
        mask1_out[...] = cleared

        @pl.when(step == 0)
        def _():
            feat_total[...] = feat_part
            targ_total[...] = targ_part

        @pl.when(step > 0)
        def _():
            feat_total[...] += feat_part
            targ_total[...] += targ_part

        @pl.when(step == pl.num_programs(0) - 1)
        def _():
            for index, flag in enumerate((first, second)):
                keep = flag > 0
                spread_out[pl.ds(index * block, block), :] = jnp.where(keep, feat_total[...], 0.0).astype(bf16)
                targ_out[pl.ds(index * block, block), :] = jnp.where(keep, targ_total[...], 0.0)


def gather_own(flags, rows, features, coefficients, targets):
    count, width = features.shape
    outs = coefficients.shape[1]
    block = rows.shape[0]
    tile = min(1024, count)
    moving = lambda columns: pl.BlockSpec((tile, columns), lambda i: (i, 0))
    still = lambda shape: pl.BlockSpec(shape, lambda i: (0, 0))
    return pl.pallas_call(
        gather_kernel,
        grid=(count // tile,),
        in_specs=[whole_smem, still((block, 1)), still((1, block)), moving(width), moving(outs), moving(outs)],
        out_specs=[
            still((2 * block, width)), still((2 * block, outs)), moving(outs), moving(outs),
            pl.BlockSpec((1, tile), lambda i: (0, i)),
        ],
        out_shape=[
            jax.ShapeDtypeStruct((2 * block, width), bf16), jax.ShapeDtypeStruct((2 * block, outs), f32),
            jax.ShapeDtypeStruct((count, outs), bf16), jax.ShapeDtypeStruct((count, outs), bf16),
            jax.ShapeDtypeStruct((1, count), f32),
        ],
        scratch_shapes=[pltpu.VMEM((block, width), f32), pltpu.VMEM((block, outs), f32)],
        compiler_params=pltpu.CompilerParams(vmem_limit_bytes=40 << 20),
        name="gather_own",
    )(flags, rows[:, None], rows[None, :], features, coefficients, targets)


def terms_kernel(arrived, feats, squares, mask0, mask1, own, terms_out, offsets):
    step = pl.program_id(0)
    width = feats.shape[1]
    block = arrived.shape[0] // 2
    scale = math.log2(math.e) / width

    @pl.when(step == 0)
    def _():
        offsets[...] = row_squares(arrived[...]) * (-scale)
        terms_out[...] = own[...]

    beside = squares[...] * (-scale)
    piece = block // 2
    for part in range(4):
        span = pl.ds(part * piece, piece)
        products = nt_dot(arrived[span, :], feats[...])
        values = jnp.exp2(products * (2.0 * scale) + offsets[span, :] + beside).astype(bf16)
        mask = mask0 if part < 2 else mask1
        terms_out[span, :] -= nn_dot(values, mask[...])


def local_terms(arrived, features, squares, mask0, mask1, own):
    count, width = features.shape
    outs = own.shape[1]
    tile = min(1024, count)
    moving = lambda columns: pl.BlockSpec((tile, columns), lambda i: (i, 0))
    still = lambda shape: pl.BlockSpec(shape, lambda i: (0, 0))
    return pl.pallas_call(
        terms_kernel,
        grid=(count // tile,),
        in_specs=[
            still(arrived.shape), moving(width), pl.BlockSpec((1, tile), lambda i: (0, i)), moving(outs), moving(outs),
            still(own.shape),
        ],
        out_specs=still(own.shape),
        out_shape=jax.ShapeDtypeStruct(own.shape, f32),
        scratch_shapes=[pltpu.VMEM((arrived.shape[0], 1), f32)],
        compiler_params=pltpu.CompilerParams(vmem_limit_bytes=40 << 20),
        name="local_terms",
    )(arrived, features, squares, mask0, mask1, own)


def newton_plan(size):
    least, most = ridge_term * 0.96, size + ridge_term + 0.1
    radius = (most - least) / (most + least)
    start = 2.0 / (most + least)
    scales = []
    for _ in range(newton_steps):
        scales.append(2.0 / (2.0 - radius * radius))
        radius = radius * radius / (2.0 - radius * radius)
    return start, scales


def invert_pair(matrices, keep):
    size = matrices[0].shape[0]
    start, scales = newton_plan(size)
    eye = jnp.where(
        lax.broadcasted_iota(jnp.int32, (size, size), 0) == lax.broadcasted_iota(jnp.int32, (size, size), 1), 1.0, 0.0
    )
    for index, matrix in enumerate(matrices):
        keep[index] = (2.0 * start * scales[0]) * eye - (start * start * scales[0]) * matrix
    for scale in scales[1:]:
        guesses = [keep[index] for index in range(2)]
        rests = [fine_dot(matrix, guess) for matrix, guess in zip(matrices, guesses)]
        for index in range(2):
            change = fine_dot(guesses[index], rests[index])
            keep[index] = (2.0 * scale) * guesses[index] - scale * change


def factor_kernel(arrived, first_out, cross_out, second_out, between_out):
    width = arrived.shape[1]
    block = arrived.shape[0] // 2
    half = block // 2
    scale = math.log2(math.e) / width

    def values(left, right):
        left_rows, right_rows = arrived[left, :], arrived[right, :]
        distance = row_squares(left_rows) + lane_squares(right_rows) - 2.0 * nt_dot(left_rows, right_rows)
        return jnp.exp2(distance * (-scale))

    span = lambda index, part: pl.ds(index * block + part * half, half)
    ridge = jnp.where(
        lax.broadcasted_iota(jnp.int32, (half, half), 0) == lax.broadcasted_iota(jnp.int32, (half, half), 1),
        ridge_term, 0.0,
    )
    invert_pair([values(span(i, 0), span(i, 0)) + ridge for i in range(2)], first_out)
    rests = []
    for i in range(2):
        low = values(span(i, 1), span(i, 0))
        cross = fine_dot(low, first_out[i])
        cross_out[i] = cross
        rests.append(values(span(i, 1), span(i, 1)) + ridge - fine_dot(cross, low, nt_dot))
    invert_pair(rests, second_out)
    for part in range(2):
        between_out[pl.ds(part * half, half), :] = values(span(1, part), pl.ds(0, block)).astype(bf16)


def factor(arrived):
    block = arrived.shape[0] // 2
    half = block // 2
    shape = jax.ShapeDtypeStruct((2, half, half), f32)
    return pl.pallas_call(
        factor_kernel,
        in_specs=[whole_vmem],
        out_specs=[whole_vmem] * 4,
        out_shape=[shape, shape, shape, jax.ShapeDtypeStruct((block, block), bf16)],
        compiler_params=pltpu.CompilerParams(vmem_limit_bytes=40 << 20),
        name="factor",
    )(arrived)


def finish_kernel(flags, rows_across, coefs, sides, first_inv, cross, second_inv, between, out, pieces):
    step = pl.program_id(0)
    block = rows_across.shape[1]
    half = block // 2
    tile, outs = coefs.shape

    def solve(index, upper, lower):
        rest = lower - fine_dot(cross[index], upper)
        low_part = fine_dot(second_inv[index], rest)
        high_part = fine_dot(first_inv[index], upper) - fine_dot(cross[index], low_part, tn_dot)
        return high_part, low_part

    mine = flags[0] + flags[1] > 0

    @pl.when(mine & (step == 0))
    def _():
        fresh = solve(0, sides[pl.ds(0, half), :], sides[pl.ds(half, half), :])
        sent = jnp.concatenate([part.astype(bf16) for part in fresh], axis=0)
        moved = nn_dot(between[...], sent)
        later = solve(1, sides[pl.ds(block, half), :] - moved[:half], sides[pl.ds(block + half, half), :] - moved[half:])
        for part in range(2):
            value = jnp.where(flags[0] > 0, fresh[part], later[part])
            high = value.astype(bf16)
            rest = value - high.astype(f32)
            mid = rest.astype(bf16)
            low = (rest - mid.astype(f32)).astype(bf16)
            for index, piece in enumerate((high, mid, low)):
                pieces[pl.ds(part * half, half), pl.ds(index * outs, outs)] = piece
        pieces[:, pl.ds(3 * outs, outs)] = jnp.ones((block, outs), bf16)

    @pl.when(mine)
    def _():
        subs = lax.broadcasted_iota(jnp.int32, (tile, block), 0) + step * tile
        place = jnp.where(subs == rows_across[...], 1.0, 0.0).astype(bf16)
        spread = nn_dot(place, pieces[...])
        value = spread[:, :outs] + spread[:, outs : 2 * outs] + spread[:, 2 * outs : 3 * outs]
        out[...] = jnp.where(spread[:, 3 * outs :] > 0.5, value, coefs[...])

    @pl.when(jnp.logical_not(mine))
    def _():
        out[...] = coefs[...]


def finish(flags, rows, coefficients, sides, first_inv, cross, second_inv, between):
    count, outs = coefficients.shape
    block = rows.shape[0]
    tile = min(1024, count)
    moving = pl.BlockSpec((tile, outs), lambda i: (i, 0))
    return pl.pallas_call(
        finish_kernel,
        grid=(count // tile,),
        in_specs=[whole_smem, whole_vmem, moving] + [whole_vmem] * 5,
        out_specs=moving,
        out_shape=jax.ShapeDtypeStruct(coefficients.shape, f32),
        scratch_shapes=[pltpu.VMEM((block, 4 * outs), bf16)],
        compiler_params=pltpu.CompilerParams(vmem_limit_bytes=40 << 20),
        name="finish",
    )(flags, rows[None, :], coefficients, sides, first_inv, cross, second_inv, between)


def per_device(features, coefficients, targets, block_rows, block_owner):
    device = lax.axis_index("wide") * lax.axis_size("narrow") + lax.axis_index("narrow")
    flags = (block_owner == device).astype(jnp.int32)
    rows = jnp.where(flags[0] > 0, block_rows[0], block_rows[1])
    spread, own, mask0, mask1, squares = gather_own(flags, rows, features, coefficients, targets)
    sizes = lax.axis_size("wide"), lax.axis_size("narrow")
    arrived = cube_sum(spread, *sizes, 0)
    terms = local_terms(arrived, features, squares, mask0, mask1, own)
    sides = cube_sum(terms, *sizes, 1)
    parts = factor(arrived)
    return finish(flags, rows, coefficients, sides, *parts)


def solution(mesh):
    rows = P(("wide", "narrow"), None)
    return jax.shard_map(
        per_device,
        mesh=mesh,
        in_specs=(rows, rows, rows, P(), P()),
        out_specs=rows,
        check_vma=False,
    )
```

```python
import functools
import math

import jax
import jax.numpy as jnp
from jax import lax
from jax.experimental import pallas as pl
from jax.experimental.pallas import tpu as pltpu
from jax.sharding import PartitionSpec as P

ridge_term = 0.5
newton_steps = 8
f32 = jnp.float32
bf16 = jnp.bfloat16
whole_vmem = pl.BlockSpec(memory_space=pltpu.VMEM)
whole_smem = pl.BlockSpec(memory_space=pltpu.SMEM)


def nn_dot(left, right):
    return jnp.dot(left, right, preferred_element_type=f32)


def nt_dot(left, right):
    return lax.dot_general(left, right, (((1,), (1,)), ((), ())), preferred_element_type=f32)


def tn_dot(left, right):
    return lax.dot_general(left, right, (((0,), (0,)), ((), ())), preferred_element_type=f32)


def halves(value):
    high = value.astype(bf16)
    return high, (value - high.astype(f32)).astype(bf16)


def fine_dot(left, right, dot=nn_dot):
    left_high, left_low = halves(left)
    right_high, right_low = halves(right)
    return dot(left_high, right_high) + (dot(left_high, right_low) + dot(left_low, right_high))


def row_squares(rows):
    widened = rows.astype(f32)
    return jnp.sum(widened * widened, axis=1, keepdims=True)


def lane_squares(rows):
    widened = rows.astype(f32)
    high, low = halves(widened * widened)
    ones = jnp.ones((8, rows.shape[1]), bf16)
    return (nt_dot(ones, high) + nt_dot(ones, low))[0:1]


def cube_orders(wide, narrow, parts):
    bits = [("narrow", 1 << k) for k in range(narrow.bit_length() - 1)]
    bits += [("wide", 1 << k) for k in range(wide.bit_length() - 1)]
    inner = bits[1:-1]
    turned = [bits[:1] + inner[turn:] + inner[:turn] + bits[-1:] for turn in range(max(len(inner), 1))]
    return [turned[part % len(turned)] for part in range(parts)]


def cube_kernel(orders, extra, value, *refs):
    steps = len(orders[0])
    if extra:
        arrived, out, *results = refs[:6]
        scratch = refs[6:]
        work = factor_pieces(arrived, *results)
    else:
        out, *scratch = refs
        work = iter(())
    share = 2
    kept, sems = scratch[:-1], scratch[-1]
    chunks = 1 << steps

    def side(bit):
        axis, weight = bit
        return lax.rem(lax.axis_index(axis) // weight, 2)

    def partner(bit):
        axis, weight = bit
        place = {name: lax.axis_index(name) for name in ("wide", "narrow")}
        place[axis] = place[axis] + weight - 2 * weight * side(bit)
        return (place["wide"], place["narrow"])

    def copy(source, target, bit, part, step, phase):
        return pltpu.make_async_remote_copy(
            src_ref=source, dst_ref=target, send_sem=sems.at[0, phase, part, step], recv_sem=sems.at[1, phase, part, step],
            device_id=partner(bit), device_id_type=pl.DeviceIdType.MESH,
        )

    barrier = pltpu.get_barrier_semaphore()
    for bit in orders[0]:
        pl.semaphore_signal(barrier, inc=1, device_id=partner(bit), device_id_type=pl.DeviceIdType.MESH)
    pl.semaphore_wait(barrier, steps)

    def held(part, step):
        if step < 0:
            return value.at[pl.ds(part * chunks, chunks)]
        return kept[part * steps + step]

    started = []
    flying = {}

    def absorb(part, step):
        count = chunks >> (step + 1)
        flying[part].wait_recv()
        spot = held(part, step)
        spot[...] = spot[...] + held(part, step - 1)[pl.ds(side(orders[part][step]) * count, count)]

    for step in range(steps):
        count = chunks >> (step + 1)
        for part, order in enumerate(orders):
            if step > 0:
                absorb(part, step - 1)
            away = (1 - side(order[step])) * count
            flying[part] = copy(held(part, step - 1).at[pl.ds(away, count)], held(part, step), order[step], part, step, 0)
            flying[part].start()
            started.append(flying[part])
        for _ in range(share):
            next(work, None)
    bases = []
    for part, order in enumerate(orders):
        absorb(part, steps - 1)
        base = part * chunks
        listed = []
        for step in range(steps):
            base = base + side(order[step]) * (chunks >> (step + 1))
            listed.append(base)
        bases.append(listed)
        out[pl.ds(base, 1)] = held(part, steps - 1)[...]
    for step in reversed(range(steps)):
        count = chunks >> (step + 1)
        for part, order in enumerate(orders):
            if step < steps - 1:
                flying[part].wait_recv()
            span = out.at[pl.ds(bases[part][step], count)]
            flying[part] = copy(span, span, order[step], part, step, 1)
            flying[part].start()
            started.append(flying[part])
        for _ in range(share):
            next(work, None)
    for _ in work:
        pass
    for part in range(len(orders)):
        flying[part].wait_recv()
    for sent in started:
        sent.wait_send()


def cube_sum(value, wide, narrow, number, arrived=None):
    rows, columns = value.shape
    chunks = wide * narrow
    parts = 4 if rows // (4 * chunks) >= 8 else 2
    orders = cube_orders(wide, narrow, parts)
    steps = len(orders[0])
    depth = rows // (parts * chunks)
    shape = (parts * chunks, depth, columns)
    slots = [pltpu.VMEM((chunks >> (step + 1), depth, columns), value.dtype) for _ in orders for step in range(steps)]
    extra = () if arrived is None else (arrived,)
    shapes = [jax.ShapeDtypeStruct(shape, value.dtype)]
    if extra:
        block = arrived.shape[0] // 2
        square = jax.ShapeDtypeStruct((2, block // 2, block // 2), f32)
        shapes += [square, square, square, jax.ShapeDtypeStruct((block, block), bf16)]
    summed, *results = pl.pallas_call(
        functools.partial(cube_kernel, orders, bool(extra)),
        in_specs=[whole_vmem] * (1 + len(extra)),
        out_specs=[whole_vmem] * len(shapes),
        out_shape=shapes,
        scratch_shapes=slots + [pltpu.SemaphoreType.DMA((2, 2, parts, steps))],
        compiler_params=pltpu.CompilerParams(collective_id=number, has_side_effects=True, vmem_limit_bytes=40 << 20),
        name="cube_sum",
    )(value.reshape(shape), *extra)
    return summed.reshape(rows, columns), results


def own_flags(owners):
    device = lax.axis_index("wide") * lax.axis_size("narrow") + lax.axis_index("narrow")
    return [jnp.where(owners[index] == device, 1, 0) for index in range(2)]


def place_rows(first, listed, tile, step):
    block = listed.shape[1]
    rows = jnp.where(first > 0, listed[0:1, :], listed[1:2, :])
    subs = lax.broadcasted_iota(jnp.int32, (tile, block), 0) + step * tile
    return jnp.where(subs == rows, 1.0, 0.0).astype(bf16)


def gather_kernel(owners, listed, feats, coefs, targs, spread_out, targ_out, mask0_out, mask1_out,
                  squares_out, feat_total, targ_total):
    step = pl.program_id(0)
    tile = feats.shape[0]
    block = listed.shape[1]
    first, second = own_flags(owners)
    squares_out[...] = lane_squares(feats[...])
    plain = coefs[...].astype(bf16)

    @pl.when(first + second == 0)
    def _():
        mask0_out[...] = plain
        mask1_out[...] = plain

        @pl.when(step == 0)
        def _():
            spread_out[...] = jnp.zeros_like(spread_out)
            targ_out[...] = jnp.zeros_like(targ_out)

    @pl.when(first + second > 0)
    def _():
        place = place_rows(first, listed, tile, step)
        feat_part = tn_dot(place, feats[...])
        targ_part = tn_dot(place, targs[...])
        taken = nn_dot(place, jnp.ones((block, coefs.shape[1]), bf16)) > 0.5
        cleared = jnp.where(taken, 0.0, coefs[...]).astype(bf16)
        mask0_out[...] = jnp.where(first > 0, cleared, plain)
        mask1_out[...] = cleared

        @pl.when(step == 0)
        def _():
            feat_total[...] = feat_part
            targ_total[...] = targ_part

        @pl.when(step > 0)
        def _():
            feat_total[...] += feat_part
            targ_total[...] += targ_part

        @pl.when(step == pl.num_programs(0) - 1)
        def _():
            for index, flag in enumerate((first, second)):
                keep = flag > 0
                spread_out[pl.ds(index * block, block), :] = jnp.where(keep, feat_total[...], 0.0).astype(bf16)
                targ_out[pl.ds(index * block, block), :] = jnp.where(keep, targ_total[...], 0.0)


def gather_own(owners, listed, features, coefficients, targets):
    count, width = features.shape
    outs = coefficients.shape[1]
    block = listed.shape[1]
    tile = min(1024, count)
    moving = lambda columns: pl.BlockSpec((tile, columns), lambda i: (i, 0))
    still = lambda shape: pl.BlockSpec(shape, lambda i: (0, 0))
    return pl.pallas_call(
        gather_kernel,
        grid=(count // tile,),
        in_specs=[whole_smem, still(listed.shape), moving(width), moving(outs), moving(outs)],
        out_specs=[
            still((2 * block, width)), still((2 * block, outs)), moving(outs), moving(outs),
            pl.BlockSpec((1, tile), lambda i: (0, i)),
        ],
        out_shape=[
            jax.ShapeDtypeStruct((2 * block, width), bf16), jax.ShapeDtypeStruct((2 * block, outs), f32),
            jax.ShapeDtypeStruct((count, outs), bf16), jax.ShapeDtypeStruct((count, outs), bf16),
            jax.ShapeDtypeStruct((1, count), f32),
        ],
        scratch_shapes=[pltpu.VMEM((block, width), f32), pltpu.VMEM((block, outs), f32)],
        compiler_params=pltpu.CompilerParams(vmem_limit_bytes=58 << 20),
        name="gather_own",
    )(owners, listed, features, coefficients, targets)


def terms_kernel(arrived, feats, squares, mask0, mask1, own, terms_out, offsets):
    step = pl.program_id(0)
    width = feats.shape[1]
    block = arrived.shape[0] // 2
    scale = math.log2(math.e) / width

    @pl.when(step == 0)
    def _():
        offsets[...] = row_squares(arrived[...]) * (-scale)
        terms_out[...] = own[...]

    beside = squares[...] * (-scale)
    piece = block // 2
    for part in range(4):
        span = pl.ds(part * piece, piece)
        products = nt_dot(arrived[span, :], feats[...])
        values = jnp.exp2(products * (2.0 * scale) + offsets[span, :] + beside).astype(bf16)
        mask = mask0 if part < 2 else mask1
        terms_out[span, :] -= nn_dot(values, mask[...])


def local_terms(arrived, features, squares, mask0, mask1, own):
    count, width = features.shape
    outs = own.shape[1]
    tile = min(1024, count)
    moving = lambda columns: pl.BlockSpec((tile, columns), lambda i: (i, 0))
    still = lambda shape: pl.BlockSpec(shape, lambda i: (0, 0))
    return pl.pallas_call(
        terms_kernel,
        grid=(count // tile,),
        in_specs=[
            still(arrived.shape), moving(width), pl.BlockSpec((1, tile), lambda i: (0, i)), moving(outs), moving(outs),
            still(own.shape),
        ],
        out_specs=still(own.shape),
        out_shape=jax.ShapeDtypeStruct(own.shape, f32),
        scratch_shapes=[pltpu.VMEM((arrived.shape[0], 1), f32)],
        compiler_params=pltpu.CompilerParams(vmem_limit_bytes=40 << 20),
        name="local_terms",
    )(arrived, features, squares, mask0, mask1, own)


def newton_plan(size):
    least, most = ridge_term * 0.96, size + ridge_term + 0.1
    radius = (most - least) / (most + least)
    start = 2.0 / (most + least)
    scales = []
    for _ in range(newton_steps):
        scales.append(2.0 / (2.0 - radius * radius))
        radius = radius * radius / (2.0 - radius * radius)
    return start, scales


def invert_pair(matrices, keep):
    size = matrices[0].shape[0]
    start, scales = newton_plan(size)
    eye = jnp.where(
        lax.broadcasted_iota(jnp.int32, (size, size), 0) == lax.broadcasted_iota(jnp.int32, (size, size), 1), 1.0, 0.0
    )
    for index, matrix in enumerate(matrices):
        keep[index] = (2.0 * start * scales[0]) * eye - (start * start * scales[0]) * matrix
    yield
    for scale in scales[1:]:
        guesses = [keep[index] for index in range(2)]
        rests = [fine_dot(matrix, guess) for matrix, guess in zip(matrices, guesses)]
        for index in range(2):
            change = fine_dot(guesses[index], rests[index])
            keep[index] = (2.0 * scale) * guesses[index] - scale * change
        yield


def factor_pieces(arrived, first_out, cross_out, second_out, between_out):
    width = arrived.shape[1]
    block = arrived.shape[0] // 2
    half = block // 2
    scale = math.log2(math.e) / width

    def values(left, right):
        left_rows, right_rows = arrived[left, :], arrived[right, :]
        distance = row_squares(left_rows) + lane_squares(right_rows) - 2.0 * nt_dot(left_rows, right_rows)
        return jnp.exp2(distance * (-scale))

    span = lambda index, part: pl.ds(index * block + part * half, half)
    ridge = jnp.where(
        lax.broadcasted_iota(jnp.int32, (half, half), 0) == lax.broadcasted_iota(jnp.int32, (half, half), 1),
        ridge_term, 0.0,
    )
    yield from invert_pair([values(span(i, 0), span(i, 0)) + ridge for i in range(2)], first_out)
    rests = []
    for i in range(2):
        low = values(span(i, 1), span(i, 0))
        cross = fine_dot(low, first_out[i])
        cross_out[i] = cross
        rests.append(values(span(i, 1), span(i, 1)) + ridge - fine_dot(cross, low, nt_dot))
    yield from invert_pair(rests, second_out)
    for part in range(2):
        between_out[pl.ds(part * half, half), :] = values(span(1, part), pl.ds(0, block)).astype(bf16)


def finish_kernel(owners, listed, coefs, sides, first_inv, cross, second_inv, between, out, pieces):
    step = pl.program_id(0)
    block = listed.shape[1]
    first, second = own_flags(owners)
    half = block // 2
    tile, outs = coefs.shape

    def solve(index, upper, lower):
        rest = lower - fine_dot(cross[index], upper)
        low_part = fine_dot(second_inv[index], rest)
        high_part = fine_dot(first_inv[index], upper) - fine_dot(cross[index], low_part, tn_dot)
        return high_part, low_part

    mine = first + second > 0

    @pl.when(mine & (step == 0))
    def _():
        fresh = solve(0, sides[pl.ds(0, half), :], sides[pl.ds(half, half), :])
        sent = jnp.concatenate([part.astype(bf16) for part in fresh], axis=0)
        moved = nn_dot(between[...], sent)
        later = solve(1, sides[pl.ds(block, half), :] - moved[:half], sides[pl.ds(block + half, half), :] - moved[half:])
        for part in range(2):
            value = jnp.where(first > 0, fresh[part], later[part])
            high = value.astype(bf16)
            rest = value - high.astype(f32)
            mid = rest.astype(bf16)
            low = (rest - mid.astype(f32)).astype(bf16)
            for index, piece in enumerate((high, mid, low)):
                pieces[pl.ds(part * half, half), pl.ds(index * outs, outs)] = piece
        pieces[:, pl.ds(3 * outs, outs)] = jnp.ones((block, outs), bf16)

    @pl.when(mine)
    def _():
        place = place_rows(first, listed, tile, step)
        spread = nn_dot(place, pieces[...])
        value = spread[:, :outs] + spread[:, outs : 2 * outs] + spread[:, 2 * outs : 3 * outs]
        out[...] = jnp.where(spread[:, 3 * outs :] > 0.5, value, coefs[...])

    @pl.when(jnp.logical_not(mine))
    def _():
        out[...] = coefs[...]


def finish(owners, listed, coefficients, sides, first_inv, cross, second_inv, between):
    count, outs = coefficients.shape
    block = listed.shape[1]
    tile = min(1024, count)
    moving = pl.BlockSpec((tile, outs), lambda i: (i, 0))
    return pl.pallas_call(
        finish_kernel,
        grid=(count // tile,),
        in_specs=[whole_smem, whole_vmem, moving] + [whole_vmem] * 5,
        out_specs=moving,
        out_shape=jax.ShapeDtypeStruct(coefficients.shape, f32),
        scratch_shapes=[pltpu.VMEM((block, 4 * outs), bf16)],
        compiler_params=pltpu.CompilerParams(vmem_limit_bytes=40 << 20),
        name="finish",
    )(owners, listed, coefficients, sides, first_inv, cross, second_inv, between)


def per_device(features, coefficients, targets, block_rows, block_owner):
    sizes = lax.axis_size("wide"), lax.axis_size("narrow")
    spread, own, mask0, mask1, squares = gather_own(block_owner, block_rows, features, coefficients, targets)
    arrived, _ = cube_sum(spread, *sizes, 0)
    terms = local_terms(arrived, features, squares, mask0, mask1, own)
    sides, parts = cube_sum(terms, *sizes, 1, arrived)
    return finish(block_owner, block_rows, coefficients, sides, *parts)


def solution(mesh):
    rows = P(("wide", "narrow"), None)
    return jax.shard_map(
        per_device,
        mesh=mesh,
        in_specs=(rows, rows, rows, P(), P()),
        out_specs=rows,
        check_vma=False,
    )
```

```python
import functools
import math

import jax
import jax.numpy as jnp
from jax import lax
from jax.experimental import pallas as pl
from jax.experimental.pallas import tpu as pltpu
from jax.sharding import PartitionSpec as P

ridge_term = 0.5
newton_steps = 8
f32 = jnp.float32
bf16 = jnp.bfloat16
whole_vmem = pl.BlockSpec(memory_space=pltpu.VMEM)
whole_smem = pl.BlockSpec(memory_space=pltpu.SMEM)


def nn_dot(left, right):
    return jnp.dot(left, right, preferred_element_type=f32)


def nt_dot(left, right):
    return lax.dot_general(left, right, (((1,), (1,)), ((), ())), preferred_element_type=f32)


def tn_dot(left, right):
    return lax.dot_general(left, right, (((0,), (0,)), ((), ())), preferred_element_type=f32)


def halves(value):
    high = value.astype(bf16)
    return high, (value - high.astype(f32)).astype(bf16)


def fine_dot(left, right, dot=nn_dot):
    left_high, left_low = halves(left)
    right_high, right_low = halves(right)
    return dot(left_high, right_high) + (dot(left_high, right_low) + dot(left_low, right_high))


def row_squares(rows):
    widened = rows.astype(f32)
    return jnp.sum(widened * widened, axis=1, keepdims=True)


def lane_squares(rows):
    widened = rows.astype(f32)
    high, low = halves(widened * widened)
    ones = jnp.ones((8, rows.shape[1]), bf16)
    return (nt_dot(ones, high) + nt_dot(ones, low))[0:1]


def cube_orders(wide, narrow, parts):
    bits = [("narrow", 1 << k) for k in range(narrow.bit_length() - 1)]
    bits += [("wide", 1 << k) for k in range(wide.bit_length() - 1)]
    groups = [bits[:1]] + [bits[at : at + 2] for at in range(1, len(bits), 2)]
    inner = groups[1:]
    return [groups[:1] + inner[part % len(inner) :] + inner[: part % len(inner)] for part in range(parts)]


def cube_counts(order, chunks):
    counts = []
    for group in order:
        chunks = chunks >> len(group)
        counts.append(chunks)
    return counts


def cube_kernel(orders, chunks, extra, value, *refs):
    steps = len(orders[0])
    if extra:
        arrived, out, *results = refs[:6]
        scratch = refs[6:]
        work = factor_pieces(arrived, *results)
    else:
        out, *scratch = refs
        work = iter(())
    share = 3
    kept, sems = scratch[:-1], scratch[-1]
    counts = [cube_counts(order, chunks) for order in orders]

    def side(bit):
        axis, weight = bit
        return lax.rem(lax.axis_index(axis) // weight, 2)

    def digit(group, flip):
        total = 0
        for k, bit in enumerate(group):
            total = total + (1 - side(bit) if flip >> k & 1 else side(bit)) * (1 << k)
        return total

    def partner(group, flip):
        place = {name: lax.axis_index(name) for name in ("wide", "narrow")}
        for k, bit in enumerate(group):
            if flip >> k & 1:
                place[bit[0]] = place[bit[0]] + bit[1] - 2 * bit[1] * side(bit)
        return (place["wide"], place["narrow"])

    flips = lambda group: range(1, 1 << len(group))

    def copy(source, target, group, flip, part, step, phase):
        made = pltpu.make_async_remote_copy(
            src_ref=source, dst_ref=target, send_sem=sems.at[0, phase, part, step, flip - 1],
            recv_sem=sems.at[1, phase, part, step, flip - 1], device_id=partner(group, flip),
            device_id_type=pl.DeviceIdType.MESH,
        )
        made.start()
        return made

    barrier = pltpu.get_barrier_semaphore()
    greeted = 0
    for group in orders[0]:
        for flip in flips(group):
            pl.semaphore_signal(barrier, inc=1, device_id=partner(group, flip), device_id_type=pl.DeviceIdType.MESH)
            greeted += 1
    pl.semaphore_wait(barrier, greeted)

    def held(part, step):
        if step < 0:
            return value.at[pl.ds(part * chunks, chunks)]
        return kept[part * steps + step].at[pl.ds(0, counts[part][step])]

    started = []
    flying = {}

    def absorb(part, step):
        count = counts[part][step]
        group = orders[part][step]
        total = held(part, step - 1)[pl.ds(digit(group, 0) * count, count)]
        for flip, made in zip(flips(group), flying[part]):
            made.wait_recv()
            total = total + kept[part * steps + step][pl.ds((flip - 1) * count, count)]
        held(part, step)[...] = total

    for step in range(steps):
        for part, order in enumerate(orders):
            if step > 0:
                absorb(part, step - 1)
            group, count = order[step], counts[part][step]
            flying[part] = [
                copy(
                    held(part, step - 1).at[pl.ds(digit(group, flip) * count, count)],
                    kept[part * steps + step].at[pl.ds((flip - 1) * count, count)], group, flip, part, step, 0,
                )
                for flip in flips(group)
            ]
            started += flying[part]
        for _ in range(share):
            next(work, None)
    bases = []
    for part, order in enumerate(orders):
        absorb(part, steps - 1)
        base = part * chunks
        listed = []
        for step in range(steps):
            base = base + digit(order[step], 0) * counts[part][step]
            listed.append(base)
        bases.append(listed)
        out[pl.ds(base, 1)] = held(part, steps - 1)[...]
    for step in reversed(range(steps)):
        for part, order in enumerate(orders):
            if step < steps - 1:
                for made in flying[part]:
                    made.wait_recv()
            span = out.at[pl.ds(bases[part][step], counts[part][step])]
            flying[part] = [copy(span, span, order[step], flip, part, step, 1) for flip in flips(order[step])]
            started += flying[part]
        for _ in range(share):
            next(work, None)
    for _ in work:
        pass
    for part in range(len(orders)):
        for made in flying[part]:
            made.wait_recv()
    for sent in started:
        sent.wait_send()


def cube_sum(value, wide, narrow, number, arrived=None):
    rows, columns = value.shape
    chunks = wide * narrow
    parts = 4 if rows // (4 * chunks) >= 8 else 2
    orders = cube_orders(wide, narrow, parts)
    steps = len(orders[0])
    depth = rows // (parts * chunks)
    shape = (parts * chunks, depth, columns)
    slots = [
        pltpu.VMEM((((1 << len(group)) - 1) * count, depth, columns), value.dtype)
        for order in orders for group, count in zip(order, cube_counts(order, chunks))
    ]
    extra = () if arrived is None else (arrived,)
    shapes = [jax.ShapeDtypeStruct(shape, value.dtype)]
    if extra:
        block = arrived.shape[0] // 2
        square = jax.ShapeDtypeStruct((2, block // 2, block // 2), f32)
        shapes += [square, square, square, jax.ShapeDtypeStruct((block, block), bf16)]
    summed, *results = pl.pallas_call(
        functools.partial(cube_kernel, orders, chunks, bool(extra)),
        in_specs=[whole_vmem] * (1 + len(extra)),
        out_specs=[whole_vmem] * len(shapes),
        out_shape=shapes,
        scratch_shapes=slots + [pltpu.SemaphoreType.DMA((2, 2, parts, steps, 3))],
        compiler_params=pltpu.CompilerParams(collective_id=number, has_side_effects=True, vmem_limit_bytes=40 << 20),
        name="cube_sum",
    )(value.reshape(shape), *extra)
    return summed.reshape(rows, columns), results


def own_flags(owners):
    device = lax.axis_index("wide") * lax.axis_size("narrow") + lax.axis_index("narrow")
    return [jnp.where(owners[index] == device, 1, 0) for index in range(2)]


def place_rows(first, listed, tile, step):
    block = listed.shape[1]
    rows = jnp.where(first > 0, listed[0:1, :], listed[1:2, :])
    subs = lax.broadcasted_iota(jnp.int32, (tile, block), 0) + step * tile
    return jnp.where(subs == rows, 1.0, 0.0).astype(bf16)


def gather_kernel(owners, listed, feats, coefs, targs, spread_out, targ_out, mask0_out, mask1_out,
                  squares_out, feat_total, targ_total):
    step = pl.program_id(0)
    tile = feats.shape[0]
    block = listed.shape[1]
    first, second = own_flags(owners)
    squares_out[...] = lane_squares(feats[...])
    plain = coefs[...].astype(bf16)

    @pl.when(first + second == 0)
    def _():
        mask0_out[...] = plain
        mask1_out[...] = plain

        @pl.when(step == 0)
        def _():
            spread_out[...] = jnp.zeros_like(spread_out)
            targ_out[...] = jnp.zeros_like(targ_out)

    @pl.when(first + second > 0)
    def _():
        place = place_rows(first, listed, tile, step)
        feat_part = tn_dot(place, feats[...])
        targ_part = tn_dot(place, targs[...])
        taken = nn_dot(place, jnp.ones((block, coefs.shape[1]), bf16)) > 0.5
        cleared = jnp.where(taken, 0.0, coefs[...]).astype(bf16)
        mask0_out[...] = jnp.where(first > 0, cleared, plain)
        mask1_out[...] = cleared

        @pl.when(step == 0)
        def _():
            feat_total[...] = feat_part
            targ_total[...] = targ_part

        @pl.when(step > 0)
        def _():
            feat_total[...] += feat_part
            targ_total[...] += targ_part

        @pl.when(step == pl.num_programs(0) - 1)
        def _():
            for index, flag in enumerate((first, second)):
                keep = flag > 0
                spread_out[pl.ds(index * block, block), :] = jnp.where(keep, feat_total[...], 0.0).astype(bf16)
                targ_out[pl.ds(index * block, block), :] = jnp.where(keep, targ_total[...], 0.0)


def gather_own(owners, listed, features, coefficients, targets):
    count, width = features.shape
    outs = coefficients.shape[1]
    block = listed.shape[1]
    tile = min(1024, count)
    moving = lambda columns: pl.BlockSpec((tile, columns), lambda i: (i, 0))
    still = lambda shape: pl.BlockSpec(shape, lambda i: (0, 0))
    return pl.pallas_call(
        gather_kernel,
        grid=(count // tile,),
        in_specs=[whole_smem, still(listed.shape), moving(width), moving(outs), moving(outs)],
        out_specs=[
            still((2 * block, width)), still((2 * block, outs)), moving(outs), moving(outs),
            pl.BlockSpec((1, tile), lambda i: (0, i)),
        ],
        out_shape=[
            jax.ShapeDtypeStruct((2 * block, width), bf16), jax.ShapeDtypeStruct((2 * block, outs), f32),
            jax.ShapeDtypeStruct((count, outs), bf16), jax.ShapeDtypeStruct((count, outs), bf16),
            jax.ShapeDtypeStruct((1, count), f32),
        ],
        scratch_shapes=[pltpu.VMEM((block, width), f32), pltpu.VMEM((block, outs), f32)],
        compiler_params=pltpu.CompilerParams(vmem_limit_bytes=58 << 20),
        name="gather_own",
    )(owners, listed, features, coefficients, targets)


def terms_kernel(arrived, feats, squares, mask0, mask1, own, terms_out, offsets):
    step = pl.program_id(0)
    width = feats.shape[1]
    block = arrived.shape[0] // 2
    scale = math.log2(math.e) / width

    @pl.when(step == 0)
    def _():
        offsets[...] = row_squares(arrived[...]) * (-scale)
        terms_out[...] = own[...]

    beside = squares[...] * (-scale)
    piece = block // 2
    for part in range(4):
        span = pl.ds(part * piece, piece)
        products = nt_dot(arrived[span, :], feats[...])
        values = jnp.exp2(products * (2.0 * scale) + offsets[span, :] + beside).astype(bf16)
        mask = mask0 if part < 2 else mask1
        terms_out[span, :] -= nn_dot(values, mask[...])


def local_terms(arrived, features, squares, mask0, mask1, own):
    count, width = features.shape
    outs = own.shape[1]
    tile = min(1024, count)
    moving = lambda columns: pl.BlockSpec((tile, columns), lambda i: (i, 0))
    still = lambda shape: pl.BlockSpec(shape, lambda i: (0, 0))
    return pl.pallas_call(
        terms_kernel,
        grid=(count // tile,),
        in_specs=[
            still(arrived.shape), moving(width), pl.BlockSpec((1, tile), lambda i: (0, i)), moving(outs), moving(outs),
            still(own.shape),
        ],
        out_specs=still(own.shape),
        out_shape=jax.ShapeDtypeStruct(own.shape, f32),
        scratch_shapes=[pltpu.VMEM((arrived.shape[0], 1), f32)],
        compiler_params=pltpu.CompilerParams(vmem_limit_bytes=40 << 20),
        name="local_terms",
    )(arrived, features, squares, mask0, mask1, own)


def newton_plan(size):
    least, most = ridge_term * 0.96, size + ridge_term + 0.1
    radius = (most - least) / (most + least)
    start = 2.0 / (most + least)
    scales = []
    for _ in range(newton_steps):
        scales.append(2.0 / (2.0 - radius * radius))
        radius = radius * radius / (2.0 - radius * radius)
    return start, scales


def invert_pair(matrices, keep):
    size = matrices[0].shape[0]
    start, scales = newton_plan(size)
    eye = jnp.where(
        lax.broadcasted_iota(jnp.int32, (size, size), 0) == lax.broadcasted_iota(jnp.int32, (size, size), 1), 1.0, 0.0
    )
    for index, matrix in enumerate(matrices):
        keep[index] = (2.0 * start * scales[0]) * eye - (start * start * scales[0]) * matrix
    yield
    for scale in scales[1:]:
        guesses = [keep[index] for index in range(2)]
        rests = [fine_dot(matrix, guess) for matrix, guess in zip(matrices, guesses)]
        for index in range(2):
            change = fine_dot(guesses[index], rests[index])
            keep[index] = (2.0 * scale) * guesses[index] - scale * change
        yield


def factor_pieces(arrived, first_out, cross_out, second_out, between_out):
    width = arrived.shape[1]
    block = arrived.shape[0] // 2
    half = block // 2
    scale = math.log2(math.e) / width

    def values(left, right):
        left_rows, right_rows = arrived[left, :], arrived[right, :]
        distance = row_squares(left_rows) + lane_squares(right_rows) - 2.0 * nt_dot(left_rows, right_rows)
        return jnp.exp2(distance * (-scale))

    span = lambda index, part: pl.ds(index * block + part * half, half)
    ridge = jnp.where(
        lax.broadcasted_iota(jnp.int32, (half, half), 0) == lax.broadcasted_iota(jnp.int32, (half, half), 1),
        ridge_term, 0.0,
    )
    yield from invert_pair([values(span(i, 0), span(i, 0)) + ridge for i in range(2)], first_out)
    rests = []
    for i in range(2):
        low = values(span(i, 1), span(i, 0))
        cross = fine_dot(low, first_out[i])
        cross_out[i] = cross
        rests.append(values(span(i, 1), span(i, 1)) + ridge - fine_dot(cross, low, nt_dot))
    yield from invert_pair(rests, second_out)
    for part in range(2):
        between_out[pl.ds(part * half, half), :] = values(span(1, part), pl.ds(0, block)).astype(bf16)


def finish_kernel(owners, listed, coefs, sides, first_inv, cross, second_inv, between, out, pieces):
    step = pl.program_id(0)
    block = listed.shape[1]
    first, second = own_flags(owners)
    half = block // 2
    tile, outs = coefs.shape

    def solve(index, upper, lower):
        rest = lower - fine_dot(cross[index], upper)
        low_part = fine_dot(second_inv[index], rest)
        high_part = fine_dot(first_inv[index], upper) - fine_dot(cross[index], low_part, tn_dot)
        return high_part, low_part

    mine = first + second > 0

    @pl.when(mine & (step == 0))
    def _():
        fresh = solve(0, sides[pl.ds(0, half), :], sides[pl.ds(half, half), :])
        sent = jnp.concatenate([part.astype(bf16) for part in fresh], axis=0)
        moved = nn_dot(between[...], sent)
        later = solve(1, sides[pl.ds(block, half), :] - moved[:half], sides[pl.ds(block + half, half), :] - moved[half:])
        for part in range(2):
            value = jnp.where(first > 0, fresh[part], later[part])
            high = value.astype(bf16)
            rest = value - high.astype(f32)
            mid = rest.astype(bf16)
            low = (rest - mid.astype(f32)).astype(bf16)
            for index, piece in enumerate((high, mid, low)):
                pieces[pl.ds(part * half, half), pl.ds(index * outs, outs)] = piece
        pieces[:, pl.ds(3 * outs, outs)] = jnp.ones((block, outs), bf16)

    @pl.when(mine)
    def _():
        place = place_rows(first, listed, tile, step)
        spread = nn_dot(place, pieces[...])
        value = spread[:, :outs] + spread[:, outs : 2 * outs] + spread[:, 2 * outs : 3 * outs]
        out[...] = jnp.where(spread[:, 3 * outs :] > 0.5, value, coefs[...])

    @pl.when(jnp.logical_not(mine))
    def _():
        out[...] = coefs[...]


def finish(owners, listed, coefficients, sides, first_inv, cross, second_inv, between):
    count, outs = coefficients.shape
    block = listed.shape[1]
    tile = min(1024, count)
    moving = pl.BlockSpec((tile, outs), lambda i: (i, 0))
    return pl.pallas_call(
        finish_kernel,
        grid=(count // tile,),
        in_specs=[whole_smem, whole_vmem, moving] + [whole_vmem] * 5,
        out_specs=moving,
        out_shape=jax.ShapeDtypeStruct(coefficients.shape, f32),
        scratch_shapes=[pltpu.VMEM((block, 4 * outs), bf16)],
        compiler_params=pltpu.CompilerParams(vmem_limit_bytes=40 << 20),
        name="finish",
    )(owners, listed, coefficients, sides, first_inv, cross, second_inv, between)


def per_device(features, coefficients, targets, block_rows, block_owner):
    sizes = lax.axis_size("wide"), lax.axis_size("narrow")
    spread, own, mask0, mask1, squares = gather_own(block_owner, block_rows, features, coefficients, targets)
    arrived, _ = cube_sum(spread, *sizes, 0)
    terms = local_terms(arrived, features, squares, mask0, mask1, own)
    sides, parts = cube_sum(terms, *sizes, 1, arrived)
    return finish(block_owner, block_rows, coefficients, sides, *parts)


def solution(mesh):
    rows = P(("wide", "narrow"), None)
    return jax.shard_map(
        per_device,
        mesh=mesh,
        in_specs=(rows, rows, rows, P(), P()),
        out_specs=rows,
        check_vma=False,
    )
```
